32 devices in a mesh: space: 8 (over z, y), chan: 4 (over x, core).
Axes of the slice: x: 2, y: 2, z: 4, core: 2. Of those that a mesh axis runs over, the one named last changes fastest.
Arguments:
- features: bfloat16 [128, 64, 128], P('space'), may hold values from -6 to 6
- neighbours: int32 [128, 26], P('space'), may hold values from -1 to 127, as said below
- parent_index: int32 [128], P('space'), may hold values from 0 to 31, as said below
- octant: int32 [128], P('space'), may hold values from 0 to 7, as said below
- parent_dest: int32 [32], P('space'), may hold values from 0 to 63, as said below
- conv_fine: bfloat16 [128, 3456], P('chan'), may hold values from -0.109375 to 0.109375
- conv_down: bfloat16 [256, 3456], P('chan'), may hold values from -0.15625 to 0.15625
- conv_coarse: bfloat16 [256, 6912], P('chan'), may hold values from -0.15625 to 0.15625
- norm_gain: float32 [256], P('chan'), may hold values from 0.25 to 1.75
Outputs:
- coarse_parents: bfloat16 [256, 4096], P('chan', 'space')
The draws below stay inside these ranges and needn't reach their ends.
Inputs may be any that keep to these rules, and one draw needn't show every extreme that they name: Brick n lies on device n // 16 of space. Device d holds 16 distinct positions of a slab of 2 x 4 x 4 brick positions (x = 2 d or 2 d + 1, y, z); brick n's position gives parent_index[n] = d * 4 + (y // 2) * 2 + z // 2 and octant[n] = x % 2 + 2 (y % 2) + 4 (z % 2). neighbours[n, k] is the brick at the k-th offset (a, b, c), a, b, c in -1, 0, 1, (0, 0, 0) left out, in increasing 9 a + 3 b + c, or -1 where that position holds no brick. `parent_index`: as stated for neighbours. `octant`: as stated for neighbours. parent_dest[g] = owner * 8 + slot, where the owner of a parent of device d is d - 1, d or d + 1. At most 2 parents of one device go to each of its two neighbours, and some device sends 2 to a neighbour; some owner receives 8 parents. An owner's slots are filled from 0 upward without gaps, in order of source device and then of parent.
All inputs are finite; a program needn't handle non-finite values.
Results may differ from the reference program's by a relative error of at most 0.0065.
Values may be sent and summed in bfloat16 or wider, within the bound.
A program may use at most 64 MiB of HBM per device.

```python
import jax
import jax.numpy as jnp
from jax import lax

FINE_CH = 128
COARSE_CH = 256
EDGE = 4
SLAB_Y = 4
SLAB_Z = 4
BRICK_DEV = 16
PARENT_DEV = 4
SLOTS_DEV = 8
BRICKS = 128
N_SPACE = 8


offset_list = [(a, b, c) for a in (-1, 0, 1) for b in (-1, 0, 1) for c in (-1, 0, 1)]


around_list = [item for item in offset_list if item != (0, 0, 0)]


def geometry(key):
    devices = N_SPACE
    places = 2 * SLAB_Y * SLAB_Z
    keys = jax.random.split(jax.random.fold_in(key, 17), devices)
    chosen = jax.vmap(lambda subkey: jax.random.permutation(subkey, places)[:BRICK_DEV])(keys).astype(jnp.int32)
    device_ids = jnp.arange(devices, dtype=jnp.int32)[:, None] * jnp.ones((1, BRICK_DEV), jnp.int32)
    x_all = 2 * device_ids + chosen % 2
    y_all = chosen // 2 % SLAB_Y
    z_all = chosen // (2 * SLAB_Y)
    width_x = 2 * devices
    brick_ids = jnp.arange(devices * BRICK_DEV, dtype=jnp.int32)
    lookup = jnp.full((width_x * SLAB_Y * SLAB_Z,), -1, jnp.int32)
    flat_pos = (x_all + width_x * (y_all + SLAB_Y * z_all)).reshape(-1)
    lookup = lookup.at[flat_pos].set(brick_ids)
    x_flat = x_all.reshape(-1)
    y_flat = y_all.reshape(-1)
    z_flat = z_all.reshape(-1)
    columns = []
    for a, b, c in around_list:
        next_x = x_flat + a
        next_y = y_flat + b
        next_z = z_flat + c
        inside = (next_x >= 0) & (next_x < width_x) & (next_y >= 0) & (next_y < SLAB_Y) & (next_z >= 0) & (next_z < SLAB_Z)
        spot_index = jnp.where(inside, next_x + width_x * (next_y + SLAB_Y * next_z), 0)
        columns.append(jnp.where(inside, lookup[spot_index], -1))
    neighbour_table = jnp.stack(columns, 1).astype(jnp.int32)
    parent_ids = device_ids * PARENT_DEV + y_all // 2 * (SLAB_Z // 2) + z_all // 2
    octant_ids = chosen % 2 + 2 * (y_all % 2) + 4 * (z_all % 2)
    return (neighbour_table, parent_ids.reshape(-1).astype(jnp.int32), octant_ids.reshape(-1).astype(jnp.int32))


def draw_neighbours(key, part):
    return geometry(key)[0]


def draw_parent_index(key, part):
    return geometry(key)[1]


def draw_octant(key, part):
    return geometry(key)[2]


def draw_parent_dest(key, part):
    devices = N_SPACE
    parent_count = PARENT_DEV
    capacity = parent_count // 2
    slots_dev = parent_count + 2 * capacity
    first_key, second_key, third_key = jax.random.split(jax.random.fold_in(key, 29), 3)
    device_ids = jnp.arange(devices, dtype=jnp.int32)
    to_lower = jax.random.randint(first_key, (devices,), 0, capacity + 1, dtype=jnp.int32)
    to_upper = jax.random.randint(second_key, (devices,), 0, capacity + 1, dtype=jnp.int32)
    to_lower = jnp.where(device_ids == 0, 0, to_lower)
    to_upper = jnp.where(device_ids == devices - 1, 0, to_upper)
    centre = jax.random.randint(third_key, (), 1, devices - 1, dtype=jnp.int32)
    to_lower = jnp.where(device_ids == centre, 0, to_lower)
    to_upper = jnp.where(device_ids == centre, 0, to_upper)
    to_upper = jnp.where(device_ids == centre - 1, capacity, to_upper)
    to_lower = jnp.where(device_ids == centre + 1, capacity, to_lower)
    kept = parent_count - to_lower - to_upper
    zero_one = jnp.zeros((1,), jnp.int32)
    upper_prev = jnp.concatenate([zero_one, to_upper[:-1]])
    kept_prev = jnp.concatenate([zero_one, kept[:-1]])
    upper_prev_two = jnp.concatenate([zero_one, zero_one, to_upper[:-2]])
    order_ids = jnp.arange(parent_count, dtype=jnp.int32)[None, :]
    lower_count = to_lower[:, None]
    upper_count = to_upper[:, None]
    goes_lower = order_ids < lower_count
    goes_upper = order_ids >= parent_count - upper_count
    owner = jnp.where(goes_lower, device_ids[:, None] - 1, jnp.where(goes_upper, device_ids[:, None] + 1, device_ids[:, None]))
    slot = jnp.where(goes_lower, upper_prev_two[:, None] + kept_prev[:, None] + order_ids, jnp.where(goes_upper, order_ids - (parent_count - upper_count), upper_prev[:, None] + order_ids - lower_count))
    return (owner * slots_dev + slot).reshape(-1).astype(jnp.int32)


def steps_of(key, dims, cuts, least, largest):
    loudness, own = 1.0, jax.random.fold_in(key, 6)
    for dim, parts in cuts:
        draws = jnp.exp(jax.random.uniform(jax.random.fold_in(own, dim), (parts,), jnp.float32, least / len(cuts), largest / len(cuts)))
        loudness = loudness * jnp.repeat(draws, dims[dim] // parts).reshape([-1 if axis == dim else 1 for axis in range(len(dims))])
    return loudness


def normal_values(key, dims, spread, most, cuts=(), held_as=jnp.bfloat16):
    gain = steps_of(key, dims, cuts, -0.22, 0.18) if cuts else 1.0
    values = jax.random.normal(key, dims, jnp.float32) * spread * gain
    return jnp.minimum(jnp.maximum(values, -most), most).astype(held_as)


def setup_inputs(seed: int = 0) -> dict:
    key_of = jax.random.split(jax.random.key(seed), 10)
    return {
        "features": normal_values(key_of[0], (BRICKS, EDGE ** 3, FINE_CH), 1.0, 6.0, ((0, 8),)),
        "neighbours": draw_neighbours(jax.random.fold_in(key_of[9], 71), 0),
        "parent_index": draw_parent_index(jax.random.fold_in(key_of[9], 71), 0),
        "octant": draw_octant(jax.random.fold_in(key_of[9], 71), 0),
        "parent_dest": draw_parent_dest(jax.random.fold_in(key_of[9], 71), 0),
        "conv_fine": normal_values(key_of[5], (FINE_CH, 27 * FINE_CH), (27 * FINE_CH) ** -0.5, 0.109375, ((0, 4),)),
        "conv_down": normal_values(key_of[6], (COARSE_CH, 27 * FINE_CH), (27 * FINE_CH // 2) ** -0.5, 0.15625, ((0, 4),)),
        "conv_coarse": normal_values(key_of[7], (COARSE_CH, 27 * COARSE_CH), (27 * COARSE_CH // 4) ** -0.5, 0.15625, ((0, 4),)),
        "norm_gain": jnp.clip(1.0 + 0.15 * jax.random.normal(key_of[8], (COARSE_CH,), jnp.float32), 0.25, 1.75),
    }


offset_list = [(a, b, c) for a in (-1, 0, 1) for b in (-1, 0, 1) for c in (-1, 0, 1)]
around_list = [item for item in offset_list if item != (0, 0, 0)]
epsilon = 1e-06

def stride_span(first, number, stride):
    return slice(first, first + stride * (number - 1) + 1, stride)

def source_span(offset, length):
    if offset < 0:
        return slice(length - 1, length)
    if offset == 0:
        return slice(0, length)
    return slice(0, 1)

def target_span(offset, length):
    if offset < 0:
        return slice(0, 1)
    if offset == 0:
        return slice(1, length + 1)
    return slice(length + 1, length + 2)

def apply_taps(padded, weight, counts, stride):
    in_width = padded.shape[-1]
    accumulated = None
    for t, (a, b, c) in enumerate(offset_list):
        window = padded[:, stride_span(1 + a, counts[0], stride), stride_span(1 + b, counts[1], stride), stride_span(1 + c, counts[2], stride)]
        tap_block = weight[:, t * in_width:(t + 1) * in_width]
        product = lax.dot_general(window.reshape(-1, in_width), tap_block, (((1,), (1,)), ((), ())), preferred_element_type=jnp.float32)
        accumulated = product if accumulated is None else accumulated + product
    return accumulated.reshape((padded.shape[0],) + tuple(counts) + (weight.shape[0],))

def surround_all(pool_rows, brick_block, link_rows, lower_only):
    length = brick_block.shape[1]
    padded_size = length + 1 if lower_only else length + 2
    padded = jnp.zeros((brick_block.shape[0], padded_size, padded_size, padded_size, brick_block.shape[-1]), brick_block.dtype)
    padded = padded.at[:, 1:length + 1, 1:length + 1, 1:length + 1].set(brick_block)
    blank_index = pool_rows.shape[0] - 1
    for k, (a, b, c) in enumerate(around_list):
        if lower_only and max(a, b, c) > 0:
            continue
        row_index = jnp.where(link_rows[:, k] >= 0, link_rows[:, k], blank_index).astype(jnp.int32)
        fetched = jnp.take(pool_rows, row_index, axis=0)
        fetched = fetched[:, source_span(a, length), source_span(b, length), source_span(c, length)]
        padded = padded.at[:, target_span(a, length), target_span(b, length), target_span(c, length)].set(fetched)
    return padded

def assemble_slab(pieces, local_parent, octant):
    brick_count = pieces.shape[0]
    half_edge = pieces.shape[1]
    places = 2 * SLAB_Y * SLAB_Z
    x_bit = octant % 2
    y_pos = 2 * (local_parent // (SLAB_Z // 2)) + octant // 2 % 2
    z_pos = 2 * (local_parent % (SLAB_Z // 2)) + octant // 4
    position = x_bit + 2 * y_pos + 2 * SLAB_Y * z_pos
    matches = position[None, :] == jnp.arange(places, dtype=jnp.int32)[:, None]
    brick_ids = jnp.arange(brick_count, dtype=jnp.int32)
    row_index = jnp.where(jnp.any(matches, 1), lax.optimization_barrier(jnp.sum(jnp.where(matches, brick_ids[None, :], 0), 1)), brick_count).astype(jnp.int32)
    blank_row = jnp.zeros((1,) + pieces.shape[1:], pieces.dtype)
    placed = jnp.take(jnp.concatenate([pieces, blank_row], 0), row_index, axis=0)
    placed = placed.reshape(SLAB_Z, SLAB_Y, 2, half_edge, half_edge, half_edge, pieces.shape[-1])
    placed = placed.transpose(2, 3, 1, 4, 0, 5, 6)
    return placed.reshape(2 * half_edge, SLAB_Y * half_edge, SLAB_Z * half_edge, pieces.shape[-1])

def split_parents(coarse_slab):
    edge_cells = coarse_slab.shape[0]
    rows_y = coarse_slab.shape[1] // edge_cells
    rows_z = coarse_slab.shape[2] // edge_cells
    shaped = coarse_slab.reshape(edge_cells, rows_y, edge_cells, rows_z, edge_cells, coarse_slab.shape[-1])
    shaped = shaped.transpose(1, 3, 0, 2, 4, 5)
    return shaped.reshape(rows_y * rows_z, edge_cells ** 3, coarse_slab.shape[-1])

def reference(features, neighbours, parent_index, octant, parent_dest, conv_fine, conv_down, conv_coarse, norm_gain):
    half_edge = EDGE // 2
    brick_cubes = features.reshape(N_SPACE, BRICK_DEV, EDGE, EDGE, EDGE, FINE_CH)
    link_all = neighbours.reshape(N_SPACE, BRICK_DEV, 26)
    blank_row = jnp.zeros((1, EDGE, EDGE, EDGE, FINE_CH), features.dtype)
    feature_pool = jnp.concatenate([features.reshape(-1, EDGE, EDGE, EDGE, FINE_CH), blank_row], 0)

    def fine_step(inputs):
        padded = surround_all(feature_pool, inputs[0], inputs[1], False)
        return jnp.maximum(apply_taps(padded, conv_fine, (EDGE, EDGE, EDGE), 1), 0.0).astype(jnp.bfloat16)
    hidden = lax.map(fine_step, (brick_cubes, link_all))
    hidden_pool = jnp.concatenate([hidden.reshape(-1, EDGE, EDGE, EDGE, FINE_CH), blank_row.astype(hidden.dtype)], 0)

    def down_step(inputs):
        padded = surround_all(hidden_pool, inputs[0], inputs[1], True)
        return jnp.maximum(apply_taps(padded, conv_down, (half_edge, half_edge, half_edge), 2), 0.0).astype(jnp.bfloat16)
    pieces = lax.map(down_step, (hidden, link_all))
    device_ids = jnp.arange(N_SPACE, dtype=jnp.int32)
    local_parent = parent_index.reshape(N_SPACE, BRICK_DEV) - PARENT_DEV * device_ids[:, None]
    octants = octant.reshape(N_SPACE, BRICK_DEV)
    slabs = lax.map(lambda inputs: assemble_slab(inputs[0], inputs[1], inputs[2]), (pieces, local_parent, octants))
    span_y = slabs.shape[2]
    span_z = slabs.shape[3]
    grid_all = jnp.pad(slabs.reshape(N_SPACE * EDGE, span_y, span_z, COARSE_CH), ((1, 1), (1, 1), (1, 1), (0, 0)))

    def coarse_step(device):
        window = lax.dynamic_slice_in_dim(grid_all, (device * EDGE).astype(jnp.int32), EDGE + 2, 0)
        convolved = apply_taps(window[None], conv_coarse, (EDGE, span_y, span_z), 1)[0].astype(jnp.bfloat16)
        return split_parents(convolved)
    parents = lax.map(coarse_step, device_ids).reshape(N_SPACE * PARENT_DEV, EDGE ** 3, COARSE_CH)
    values = parents.astype(jnp.float32)
    cell_power = lax.optimization_barrier(jnp.sum(values * values, -1))
    normed = (values * lax.rsqrt(cell_power[..., None] / COARSE_CH + epsilon) * norm_gain).astype(jnp.bfloat16)
    result = jnp.zeros((N_SPACE * SLOTS_DEV, EDGE ** 3, COARSE_CH), jnp.bfloat16)
    result = result.at[parent_dest].set(normed)
    return result.transpose(2, 0, 1).reshape(COARSE_CH, N_SPACE * SLOTS_DEV * EDGE ** 3)
```

```python
import functools

import jax
import jax.numpy as jnp
from jax import lax
from jax.experimental import pallas as pl
from jax.experimental.pallas import tpu as pltpu
from jax.sharding import PartitionSpec as P

EDGE = 4
SLAB_Y = 4
SLAB_Z = 4
NY = SLAB_Y * EDGE
NZ = SLAB_Z * EDGE
LAYER = NY * NZ
NX = 2 * EDGE
CY = NY // 2
CZ = NZ // 2
CLAYER = CY * CZ
CX = NX // 2
FACE = EDGE * EDGE
epsilon = 1e-06
BF = jnp.bfloat16
F32 = jnp.float32
NT = (((1,), (1,)), ((), ()))


def iota(shape, dim):
    return lax.broadcasted_iota(jnp.int32, shape, dim)


def one(cond):
    return jnp.where(cond, 1.0, 0.0).astype(BF)


def pick(a, b):
    return jnp.dot(a, b, preferred_element_type=F32)


def fused_kernel(
    n_space,
    n_chan,
    bricks,
    slots,
    feat,
    meta,
    wf,
    wd_hbm,
    wc_hbm,
    gain,
    out,
    wd,
    wc,
    fh,
    mh,
    s_buf,
    mask,
    g_buf,
    perm_h,
    perm_c,
    sel_d,
    sel_c,
    d_buf,
    c_buf,
    e_buf,
    pb,
    pw,
    ohd,
    wsem,
    s1,
    r1,
    s2,
    r2,
    hs2,
    hr2,
    s3,
    r3,
    hs3,
    hr3,
    s4,
    r4,
    ws4,
    wr4,
):
    sp = lax.axis_index("space")
    me = lax.axis_index("chan")
    has_prev = sp > 0
    has_next = sp < n_space - 1
    fine = feat.shape[2]
    wide = fine // n_chan
    parents = (SLAB_Y // 2) * (SLAB_Z // 2)
    cells = EDGE**3
    coarse_own = wd.shape[0]
    coarse = coarse_own * n_chan
    taps2 = 9

    def rc(src, dst, ss, rs, space, chan):
        return pltpu.make_async_remote_copy(
            src_ref=src,
            dst_ref=dst,
            send_sem=ss,
            recv_sem=rs,
            device_id={"space": space, "chan": chan},
            device_id_type=pl.DeviceIdType.MESH,
        )

    copy_d = pltpu.make_async_copy(wd_hbm, wd, wsem.at[0])
    copy_c = pltpu.make_async_copy(wc_hbm, wc, wsem.at[1])
    copy_d.start()
    copy_c.start()
    peers = [lax.rem(me + k, n_chan) for k in range(1, n_chan)]

    barrier = pltpu.get_barrier_semaphore()

    def greet(space, chan):
        pl.semaphore_signal(
            barrier,
            inc=1,
            device_id={"space": space, "chan": chan},
            device_id_type=pl.DeviceIdType.MESH,
        )

    for chan in peers:
        greet(sp, chan)

    @pl.when(has_prev)
    def _():
        for chan in range(n_chan):
            greet(sp - 1, chan)

    @pl.when(has_next)
    def _():
        for chan in range(n_chan):
            greet(sp + 1, chan)

    pl.semaphore_wait(
        barrier, n_chan - 1 + n_chan * (has_prev.astype(jnp.int32) + has_next.astype(jnp.int32))
    )

    up_feat = rc(feat.at[:, pl.ds((EDGE - 1) * FACE, FACE), :], fh.at[0], s1.at[0, 0], r1.at[0, 0], sp + 1, me)
    up_meta = rc(meta, mh.at[0], s1.at[0, 1], r1.at[0, 1], sp + 1, me)
    dn_feat = rc(feat.at[:, pl.ds(0, FACE), :], fh.at[1], s1.at[1, 0], r1.at[1, 0], sp - 1, me)
    dn_meta = rc(meta, mh.at[1], s1.at[1, 1], r1.at[1, 1], sp - 1, me)

    @pl.when(has_next)
    def _():
        up_meta.start()
        up_feat.start()

    @pl.when(has_prev)
    def _():
        dn_meta.start()
        dn_feat.start()

    @pl.when(jnp.logical_not(has_prev))
    def _():
        fh[0] = jnp.zeros(fh.shape[1:], BF)
        mh[0] = jnp.zeros(mh.shape[1:], jnp.int32)
        g_buf[0] = jnp.zeros(g_buf.shape[1:], BF)
        c_buf[0] = jnp.zeros(c_buf.shape[1:], BF)
        pb[0] = jnp.zeros(pb.shape[1:], BF)
        pw[0] = jnp.zeros(pw.shape[1:], F32)

    @pl.when(jnp.logical_not(has_next))
    def _():
        fh[1] = jnp.zeros(fh.shape[1:], BF)
        mh[1] = jnp.zeros(mh.shape[1:], jnp.int32)
        c_buf[CX + 1] = jnp.zeros(c_buf.shape[1:], BF)
        pb[2] = jnp.zeros(pb.shape[1:], BF)
        pw[2] = jnp.zeros(pw.shape[1:], F32)

    lanes = meta.shape[1]
    columns = bricks * FACE
    spread = jnp.where(iota((lanes, columns), 1) // FACE == iota((lanes, columns), 0), 1.0, 0.0)
    face = iota((1, columns), 1) % FACE
    row_ids = iota((LAYER, columns), 0)

    def keys_of(meta_block):
        code = jnp.dot(meta_block.astype(F32), spread, preferred_element_type=F32)[0:1].astype(jnp.int32)
        x_bit = code % 2
        y_pos = code // 2 % SLAB_Y
        z_pos = code // (2 * SLAB_Y)
        y = y_pos * EDGE + face // EDGE
        z = z_pos * EDGE + face % EDGE
        return x_bit, y, z

    def one_hot(key, x_want, c):
        x_bit, y, z = key
        fits = (x_bit == x_want) & (z - c >= 0) & (z - c < NZ)
        return one(row_ids == jnp.where(fits, y * NZ + z - c, -1))

    blank_y = jnp.zeros((NX + 2, NZ, 3 * fine), BF)
    s_buf[:, 0:NZ, :] = blank_y
    s_buf[:, NZ + LAYER : 2 * NZ + LAYER, :] = blank_y

    faces = jnp.concatenate(
        [feat[:, i * FACE : (i + 1) * FACE, :].reshape(columns, fine) for i in range(EDGE)], axis=1
    )
    key = keys_of(meta[...])
    for x in range(2):
        for c in (-1, 0, 1):
            hot = one_hot(key, x, c)
            placed = pick(hot, faces).astype(BF)
            for i in range(EDGE):
                s_buf[1 + EDGE * x + i, NZ : NZ + LAYER, (c + 1) * fine : (c + 2) * fine] = placed[
                    :, i * fine : (i + 1) * fine
                ]
            if c == 0:
                mask[x] = pick(hot, jnp.ones((columns, fine), BF))

    def hidden_layer(x):
        parts = []
        for a in (-1, 0, 1):
            for b in (-1, 0, 1):
                parts.append(s_buf[x + 1 + a, (1 + b) * NZ : (1 + b) * NZ + LAYER, :])
        total = lax.dot_general(jnp.concatenate(parts, axis=1), wf[...], NT, preferred_element_type=F32)
        total = jnp.where(mask[x // EDGE][:, 0:wide] > 0.5, jnp.maximum(total, 0.0), 0.0)
        rows = LAYER // n_chan
        packed = jnp.concatenate([total[j * rows : (j + 1) * rows] for j in range(n_chan)], axis=1)
        g_buf[x + 1, me] = packed.astype(BF)
        for k, chan in enumerate(peers):
            rc(g_buf.at[x + 1, me], g_buf.at[x + 1, me], s2.at[x, k], r2.at[x, me], sp, chan).start()

    for x in range(1, NX - 1):
        hidden_layer(x)

    def halo_layer(side):
        k = keys_of(mh[side])
        block = fh[side].reshape(columns, fine)
        for c in (-1, 0, 1):
            s_buf[0 if side == 0 else NX + 1, NZ : NZ + LAYER, (c + 1) * fine : (c + 2) * fine] = pick(
                one_hot(k, 1 - side, c), block
            ).astype(BF)

    @pl.when(has_next)
    def _():
        dn_meta.wait_recv()
        dn_feat.wait_recv()

    halo_layer(1)
    hidden_layer(NX - 1)

    @pl.when(has_next)
    def _():
        for chan in range(n_chan):
            rc(g_buf.at[NX, me], g_buf.at[0, me], hs2.at[chan], hr2.at[me], sp + 1, chan).start()

    @pl.when(has_prev)
    def _():
        up_meta.wait_recv()
        up_feat.wait_recv()

    halo_layer(0)
    hidden_layer(0)

    big = n_chan * fine
    r, q = iota((big, big), 0), iota((big, big), 1)
    perm_h[...] = one((r % fine) // wide * fine + r // fine * wide + r % wide == q)
    half = fine // coarse_own
    big2 = n_chan * fine
    perm_c[...] = one((r % fine) // coarse_own * coarse + r // fine * coarse_own + r % coarse_own == q)
    del big2

    r, q = iota((taps2 * CLAYER, LAYER), 0), iota((taps2 * CLAYER, LAYER), 1)
    bc, at = r // CLAYER, r % CLAYER
    y = 2 * (at // CZ) + bc // 3 - 1
    z = 2 * (at % CZ) + bc % 3 - 1
    sel_d[...] = one((y >= 0) & (z >= 0) & (y * NZ + z == q))
    r, q = iota((taps2 * CLAYER, CLAYER), 0), iota((taps2 * CLAYER, CLAYER), 1)
    bc, at = r // CLAYER, r % CLAYER
    par, yz = at // FACE, at % FACE
    y = par // (SLAB_Z // 2) * EDGE + yz // EDGE + bc // 3 - 1
    z = par % (SLAB_Z // 2) * EDGE + yz % EDGE + bc % 3 - 1
    sel_c[...] = one((y >= 0) & (z >= 0) & (z < CZ) & (y * CZ + z == q))

    lane_par = jnp.where(
        iota((lanes, parents * cells), 1) // cells == iota((lanes, parents * cells), 0), 1.0, 0.0
    )
    out_ids = iota((slots * cells, parents * cells), 0)
    for k in range(3):
        block = meta[...] if k == 1 else mh[k // 2]
        rel = jnp.dot(block.astype(F32), lane_par, preferred_element_type=F32)[1:2].astype(jnp.int32)
        slot = rel - (2 - k) * slots
        target = slot * cells + iota((1, parents * cells), 1) % cells
        ohd[k] = one(out_ids == jnp.where((slot >= 0) & (slot < slots), target, -1))

    for x in range(NX):
        for k in range(1, n_chan):
            src = lax.rem(me + k, n_chan)
            rc(g_buf.at[x + 1, src], g_buf.at[x + 1, src], s2.at[x, 0], r2.at[x, src], sp, src).wait_recv()

    @pl.when(has_prev)
    def _():
        for chan in range(n_chan):
            rc(g_buf.at[0, chan], g_buf.at[0, chan], hs2.at[chan], hr2.at[chan], sp - 1, chan).wait_recv()

    gathered = jnp.concatenate(
        [jnp.concatenate([g_buf[x, s] for s in range(n_chan)], axis=1) for x in range(NX + 1)], axis=0
    )
    rows = LAYER // n_chan
    spread_h = pick(gathered, perm_h[...]).astype(BF)
    layers = [
        jnp.concatenate(
            [spread_h[x * rows : (x + 1) * rows, j * fine : (j + 1) * fine] for j in range(n_chan)], axis=0
        )
        for x in range(NX + 1)
    ]
    d_buf[...] = pick(sel_d[...], jnp.concatenate(layers, axis=1)).astype(BF)

    copy_d.wait()
    stacked = []
    for x in range(CX):
        stacked.append(
            jnp.concatenate(
                [
                    d_buf[bc * CLAYER : (bc + 1) * CLAYER, (2 * x + a) * fine : (2 * x + a + 1) * fine]
                    for a in range(3)
                    for bc in range(taps2)
                ],
                axis=1,
            )
        )
    pieces = lax.dot_general(jnp.concatenate(stacked, axis=0), wd[...], NT, preferred_element_type=F32)
    crows = CLAYER // half
    for x in range(CX):
        live = pick(sel_d[4 * CLAYER : 5 * CLAYER, :], mask[x // 2].astype(BF))[:, 0:coarse_own]
        part = pieces[x * CLAYER : (x + 1) * CLAYER]
        part = jnp.where(live > 0.5, jnp.maximum(part, 0.0), 0.0)
        c_buf[x + 1, me] = jnp.concatenate(
            [part[j * crows : (j + 1) * crows] for j in range(half)], axis=1
        ).astype(BF)

    @pl.when(has_next)
    def _():
        for chan in range(n_chan):
            rc(c_buf.at[CX, me], c_buf.at[0, me], hs3.at[0, chan], hr3.at[0, me], sp + 1, chan).start()

    @pl.when(has_prev)
    def _():
        for chan in range(n_chan):
            rc(c_buf.at[1, me], c_buf.at[CX + 1, me], hs3.at[1, chan], hr3.at[1, me], sp - 1, chan).start()

    own_c = c_buf.at[pl.ds(1, CX), me]
    for k, chan in enumerate(peers):
        rc(own_c, own_c, s3.at[k], r3.at[me], sp, chan).start()
    for k in range(1, n_chan):
        src = lax.rem(me + k, n_chan)
        ref = c_buf.at[pl.ds(1, CX), src]
        rc(ref, ref, s3.at[0], r3.at[src], sp, src).wait_recv()

    @pl.when(has_prev)
    def _():
        for chan in range(n_chan):
            ref = c_buf.at[0, chan]
            rc(ref, ref, hs3.at[0, chan], hr3.at[0, chan], sp - 1, chan).wait_recv()

    @pl.when(has_next)
    def _():
        for chan in range(n_chan):
            ref = c_buf.at[CX + 1, chan]
            rc(ref, ref, hs3.at[1, chan], hr3.at[1, chan], sp + 1, chan).wait_recv()

    gathered = jnp.concatenate(
        [jnp.concatenate([c_buf[x, s] for s in range(n_chan)], axis=1) for x in range(CX + 2)], axis=0
    )
    spread_c = pick(gathered, perm_c[...]).astype(BF)
    layers = [
        jnp.concatenate(
            [spread_c[x * crows : (x + 1) * crows, j * coarse : (j + 1) * coarse] for j in range(half)], axis=0
        )
        for x in range(CX + 2)
    ]
    e_buf[...] = pick(sel_c[...], jnp.concatenate(layers, axis=1)).astype(BF)
    copy_c.wait()
    total = None
    for a in range(3):
        for bc in range(taps2):
            block = jnp.concatenate(
                [
                    e_buf[
                        bc * CLAYER + g * FACE : bc * CLAYER + (g + 1) * FACE,
                        (x + a) * coarse : (x + a + 1) * coarse,
                    ]
                    for g in range(parents)
                    for x in range(CX)
                ],
                axis=0,
            )
            t = a * taps2 + bc
            term = lax.dot_general(wc[:, t * coarse : (t + 1) * coarse], block, NT, preferred_element_type=F32)
            total = term if total is None else total + term
    rounded = total.astype(BF)
    pb[1] = rounded
    values = rounded.astype(F32)
    pw[1, me] = jnp.sum(values * values, axis=0, keepdims=True)

    for k, chan in enumerate(peers):
        rc(pw.at[1, me], pw.at[1, me], ws4.at[1, k], wr4.at[1, me], sp, chan).start()

    @pl.when(has_next)
    def _():
        rc(pb.at[1], pb.at[0], s4.at[0], r4.at[0], sp + 1, me).start()
        for chan in range(n_chan):
            rc(pw.at[1, me], pw.at[0, me], ws4.at[0, chan], wr4.at[0, me], sp + 1, chan).start()

    @pl.when(has_prev)
    def _():
        rc(pb.at[1], pb.at[2], s4.at[1], r4.at[1], sp - 1, me).start()
        for chan in range(n_chan):
            rc(pw.at[1, me], pw.at[2, me], ws4.at[2, chan], wr4.at[2, me], sp - 1, chan).start()

    own = gain.shape[1]
    gain_col = jnp.sum(
        jnp.where(iota((own, own), 0) == iota((own, own), 1), gain[...], 0.0), axis=1, keepdims=True
    )

    def normed(k):
        power = pw[k, 0]
        for s in range(1, n_chan):
            power = power + pw[k, s]
        scaled = pb[k].astype(F32) * lax.rsqrt(power / coarse + epsilon) * gain_col
        return lax.dot_general(scaled.astype(BF), ohd[k], NT, preferred_element_type=F32)

    for k in range(1, n_chan):
        src = lax.rem(me + k, n_chan)
        rc(pw.at[1, src], pw.at[1, src], ws4.at[1, 0], wr4.at[1, src], sp, src).wait_recv()
    result = normed(1)

    @pl.when(has_prev)
    def _():
        rc(pb.at[0], pb.at[0], s4.at[0], r4.at[0], sp - 1, me).wait_recv()
        for chan in range(n_chan):
            rc(pw.at[0, chan], pw.at[0, chan], ws4.at[0, chan], wr4.at[0, chan], sp - 1, chan).wait_recv()

    @pl.when(has_next)
    def _():
        rc(pb.at[2], pb.at[2], s4.at[1], r4.at[1], sp + 1, me).wait_recv()
        for chan in range(n_chan):
            rc(pw.at[2, chan], pw.at[2, chan], ws4.at[2, chan], wr4.at[2, chan], sp + 1, chan).wait_recv()

    out[...] = (result + normed(0) + normed(2)).astype(BF)

    for x in range(NX):
        for k, chan in enumerate(peers):
            rc(g_buf.at[x + 1, me], g_buf.at[x + 1, me], s2.at[x, k], r2.at[x, me], sp, chan).wait_send()
    for k, chan in enumerate(peers):
        rc(own_c, own_c, s3.at[k], r3.at[me], sp, chan).wait_send()
        rc(pw.at[1, me], pw.at[1, me], ws4.at[1, k], wr4.at[1, me], sp, chan).wait_send()

    @pl.when(has_next)
    def _():
        up_meta.wait_send()
        up_feat.wait_send()
        rc(pb.at[1], pb.at[0], s4.at[0], r4.at[0], sp + 1, me).wait_send()
        for chan in range(n_chan):
            rc(g_buf.at[NX, me], g_buf.at[0, me], hs2.at[chan], hr2.at[me], sp + 1, chan).wait_send()
            rc(c_buf.at[CX, me], c_buf.at[0, me], hs3.at[0, chan], hr3.at[0, me], sp + 1, chan).wait_send()
            rc(pw.at[1, me], pw.at[0, me], ws4.at[0, chan], wr4.at[0, me], sp + 1, chan).wait_send()

    @pl.when(has_prev)
    def _():
        dn_meta.wait_send()
        dn_feat.wait_send()
        rc(pb.at[1], pb.at[2], s4.at[1], r4.at[1], sp - 1, me).wait_send()
        for chan in range(n_chan):
            rc(c_buf.at[1, me], c_buf.at[CX + 1, me], hs3.at[1, chan], hr3.at[1, me], sp - 1, chan).wait_send()
            rc(pw.at[1, me], pw.at[2, me], ws4.at[2, chan], wr4.at[2, me], sp - 1, chan).wait_send()


def body(n_space, n_chan, features, neighbours, parent_index, octant, parent_dest, conv_fine, conv_down, conv_coarse, norm_gain):
    device = lax.axis_index("space")
    bricks, _, fine = features.shape
    parents = parent_dest.shape[0]
    slots = 2 * parents
    local = parent_index - device * parents
    y_pos = 2 * (local // (SLAB_Z // 2)) + octant // 2 % 2
    z_pos = 2 * (local % (SLAB_Z // 2)) + octant // 4
    code = octant % 2 + 2 * y_pos + 2 * SLAB_Y * z_pos
    rel = parent_dest - (device - 1) * slots
    meta = jnp.concatenate(
        [jnp.pad(code, (0, 128 - bricks))[None], jnp.pad(rel, (0, 128 - parents))[None], jnp.zeros((6, 128), jnp.int32)], 0
    )
    down = conv_down.shape[0]
    own = conv_coarse.shape[0]
    cells = EDGE**3
    coarse = down * n_chan
    vmem = pl.BlockSpec(memory_space=pltpu.VMEM)
    hbm = pl.BlockSpec(memory_space=pl.ANY)
    dma = pltpu.SemaphoreType.DMA
    big = n_chan * fine
    crows = CLAYER // (fine // down)
    return pl.pallas_call(
        functools.partial(fused_kernel, n_space, n_chan, bricks, slots),
        out_shape=jax.ShapeDtypeStruct((own, slots * cells), BF),
        in_specs=[vmem, vmem, vmem, hbm, hbm, vmem],
        out_specs=vmem,
        scratch_shapes=[
            pltpu.VMEM(conv_down.shape, BF),
            pltpu.VMEM(conv_coarse.shape, BF),
            pltpu.VMEM((2, bricks, FACE, fine), BF),
            pltpu.VMEM((2, 8, 128), jnp.int32),
            pltpu.VMEM((NX + 2, LAYER + 2 * NZ, 3 * fine), BF),
            pltpu.VMEM((2, LAYER, fine), F32),
            pltpu.VMEM((NX + 1, n_chan, LAYER // n_chan, fine), BF),
            pltpu.VMEM((big, big), BF),
            pltpu.VMEM((big, big), BF),
            pltpu.VMEM((9 * CLAYER, LAYER), BF),
            pltpu.VMEM((9 * CLAYER, CLAYER), BF),
            pltpu.VMEM((9 * CLAYER, (NX + 1) * fine), BF),
            pltpu.VMEM((CX + 2, n_chan, crows, fine), BF),
            pltpu.VMEM((9 * CLAYER, (CX + 2) * coarse), BF),
            pltpu.VMEM((3, own, parents * cells), BF),
            pltpu.VMEM((3, n_chan, 1, parents * cells), F32),
            pltpu.VMEM((3, slots * cells, parents * cells), BF),
            dma((2,)),
            dma((2, 2)),
            dma((2, 2)),
            dma((NX, n_chan - 1)),
            dma((NX, n_chan)),
            dma((n_chan,)),
            dma((n_chan,)),
            dma((n_chan - 1,)),
            dma((n_chan,)),
            dma((2, n_chan)),
            dma((2, n_chan)),
            dma((2,)),
            dma((2,)),
            dma((3, n_chan)),
            dma((3, n_chan)),
        ],
        compiler_params=pltpu.CompilerParams(collective_id=0, has_side_effects=True),
    )(features, meta, conv_fine, conv_down, conv_coarse, norm_gain.reshape(1, -1))


def solution(mesh):
    sizes = dict(mesh.shape)
    return jax.shard_map(
        functools.partial(body, sizes["space"], sizes["chan"]),
        mesh=mesh,
        in_specs=(
            P("space", None, None),
            P("space", None),
            P("space"),
            P("space"),
            P("space"),
            P("chan", None),
            P("chan", None),
            P("chan", None),
            P("chan"),
        ),
        out_specs=P("chan", "space"),
        check_vma=False,
    )
```

```python
import functools

import jax
import jax.numpy as jnp
import numpy as np
from jax import lax
from jax.experimental import pallas as pl
from jax.experimental.pallas import tpu as pltpu
from jax.sharding import PartitionSpec as P

EDGE = 4
SLAB_Y = 4
SLAB_Z = 4
NY = SLAB_Y * EDGE
NZ = SLAB_Z * EDGE
LAYER = NY * NZ
NX = 2 * EDGE
CY = NY // 2
CZ = NZ // 2
CLAYER = CY * CZ
CX = NX // 2
FACE = EDGE * EDGE
epsilon = 1e-06
BF = jnp.bfloat16
F32 = jnp.float32
NT = (((1,), (1,)), ((), ()))


def iota(shape, dim):
    return lax.broadcasted_iota(jnp.int32, shape, dim)


def one(cond):
    return jnp.where(cond, 1.0, 0.0).astype(BF)


def pick(a, b):
    return jnp.dot(a, b, preferred_element_type=F32)


def tables(n_chan, fine, coarse_own):
    def held(cond):
        return jnp.asarray(np.asarray(cond, np.float32).astype(jnp.bfloat16))

    def grid(rows, columns):
        return np.arange(rows)[:, None], np.arange(columns)[None, :]

    wide = fine // n_chan
    coarse = coarse_own * n_chan
    r, q = grid(n_chan * fine, n_chan * fine)
    perm_h = held((r % fine) // wide * fine + r // fine * wide + r % wide == q)
    perm_c = held((r % fine) // coarse_own * coarse + r // fine * coarse_own + r % coarse_own == q)
    r, q = grid(9 * CLAYER, LAYER)
    bc, at = r // CLAYER, r % CLAYER
    y = 2 * (at // CZ) + bc // 3 - 1
    z = 2 * (at % CZ) + bc % 3 - 1
    sel_d = held((y >= 0) & (z >= 0) & (y * NZ + z == q))
    r, q = grid(9 * CLAYER, CLAYER)
    bc, at = r // CLAYER, r % CLAYER
    par, yz = at // FACE, at % FACE
    y = par // (SLAB_Z // 2) * EDGE + yz // EDGE + bc // 3 - 1
    z = par % (SLAB_Z // 2) * EDGE + yz % EDGE + bc % 3 - 1
    sel_c = held((y >= 0) & (z >= 0) & (z < CZ) & (y * CZ + z == q))
    return perm_h, perm_c, sel_d, sel_c


def fused_kernel(
    n_space, n_chan, bricks, slots,
    feat_hbm, parent_hbm, octant_hbm, dest_hbm, wf_hbm, wd_hbm, wc_hbm, gain_hbm,
    perm_h_hbm, perm_c_hbm, sel_d_hbm, sel_c_hbm,
    out,
    feat, wf, gain, parent_in, octant_in, dest_in, meta, wd, wc, fh, mh, s_buf, mask, g_buf,
    perm_h, perm_c, sel_d, sel_c, d_buf, c_buf, e_buf, pb, pw, ohd,
    wsem, s1, r1, s2, r2, hs2, hr2, s3, r3, hs3, hr3, s4, r4, ws4, wr4,
):
    sp = lax.axis_index("space")
    me = lax.axis_index("chan")
    has_prev = sp > 0
    has_next = sp < n_space - 1
    fine = feat.shape[2]
    wide = fine // n_chan
    parents = dest_in.shape[1]
    cells = EDGE**3
    coarse_own = wd.shape[0]
    coarse = coarse_own * n_chan
    taps2 = 9
    half = fine // coarse_own
    crows = CLAYER // half
    rows = LAYER // n_chan

    def rc(src, dst, ss, rs, space, chan):
        return pltpu.make_async_remote_copy(
            src_ref=src,
            dst_ref=dst,
            send_sem=ss,
            recv_sem=rs,
            device_id={"space": space, "chan": chan},
            device_id_type=pl.DeviceIdType.MESH,
        )

    peers = [lax.rem(me + k, n_chan) for k in range(1, n_chan)]
    barrier = pltpu.get_barrier_semaphore()

    def greet(space, chan):
        pl.semaphore_signal(
            barrier,
            inc=1,
            device_id={"space": space, "chan": chan},
            device_id_type=pl.DeviceIdType.MESH,
        )

    @pl.when(has_prev)
    def _():
        for chan in range(n_chan):
            greet(sp - 1, chan)

    @pl.when(has_next)
    def _():
        for chan in range(n_chan):
            greet(sp + 1, chan)

    for chan in peers:
        greet(sp, chan)

    loads = [
        pltpu.make_async_copy(src, dst, wsem.at[k])
        for k, (src, dst) in enumerate(
            (
                (parent_hbm, parent_in),
                (octant_hbm, octant_in),
                (dest_hbm, dest_in),
                (feat_hbm, feat),
                (wf_hbm, wf),
                (gain_hbm, gain),
                (perm_h_hbm, perm_h),
                (sel_d_hbm, sel_d),
                (wd_hbm, wd),
                (perm_c_hbm, perm_c),
                (sel_c_hbm, sel_c),
                (wc_hbm, wc),
            )
        )
    ]
    for load in loads:
        load.start()

    @pl.when(jnp.logical_not(has_prev))
    def _():
        fh[0] = jnp.zeros(fh.shape[1:], BF)
        mh[0] = jnp.zeros(mh.shape[1:], jnp.int32)
        g_buf[0] = jnp.zeros(g_buf.shape[1:], BF)
        c_buf[0] = jnp.zeros(c_buf.shape[1:], BF)
        pb[0] = jnp.zeros(pb.shape[1:], BF)
        pw[0] = jnp.zeros(pw.shape[1:], F32)

    @pl.when(jnp.logical_not(has_next))
    def _():
        fh[1] = jnp.zeros(fh.shape[1:], BF)
        mh[1] = jnp.zeros(mh.shape[1:], jnp.int32)
        c_buf[CX + 1] = jnp.zeros(c_buf.shape[1:], BF)
        pb[2] = jnp.zeros(pb.shape[1:], BF)
        pw[2] = jnp.zeros(pw.shape[1:], F32)

    blank_y = jnp.zeros((NX + 2, NZ, 3 * fine), BF)
    s_buf[:, 0:NZ, :] = blank_y
    s_buf[:, NZ + LAYER : 2 * NZ + LAYER, :] = blank_y

    lanes = meta.shape[1]
    columns = bricks * FACE
    spread = jnp.where(iota((lanes, columns), 1) // FACE == iota((lanes, columns), 0), 1.0, 0.0)
    face = iota((1, columns), 1) % FACE
    row_ids = iota((LAYER, columns), 0)

    meta[...] = jnp.zeros(meta.shape, jnp.int32)
    for load in loads[:4]:
        load.wait()
    local = parent_in[...] - sp * parents
    octant = octant_in[...]
    y_pos = 2 * (local // (SLAB_Z // 2)) + octant // 2 % 2
    z_pos = 2 * (local % (SLAB_Z // 2)) + octant // 4
    meta[0:1, 0:bricks] = octant % 2 + 2 * y_pos + 2 * SLAB_Y * z_pos
    meta[1:2, 0:parents] = dest_in[...] - (sp - 1) * slots

    def keys_of(meta_block):
        code = jnp.dot(meta_block.astype(F32), spread, preferred_element_type=F32)[0:1].astype(jnp.int32)
        x_bit = code % 2
        y_pos = code // 2 % SLAB_Y
        z_pos = code // (2 * SLAB_Y)
        y = y_pos * EDGE + face // EDGE
        z = z_pos * EDGE + face % EDGE
        return x_bit, y, z

    def one_hot(key, x_want, c):
        x_bit, y, z = key
        fits = (x_bit == x_want) & (z - c >= 0) & (z - c < NZ)
        return one(row_ids == jnp.where(fits, y * NZ + z - c, -1))

    faces = jnp.concatenate(
        [feat[:, i * FACE : (i + 1) * FACE, :].reshape(columns, fine) for i in range(EDGE)], axis=1
    )
    key = keys_of(meta[...])
    for x in range(2):
        for c in (-1, 0, 1):
            hot = one_hot(key, x, c)
            placed = pick(hot, faces).astype(BF)
            for i in range(EDGE):
                s_buf[1 + EDGE * x + i, NZ : NZ + LAYER, (c + 1) * fine : (c + 2) * fine] = placed[
                    :, i * fine : (i + 1) * fine
                ]
            if c == 0:
                mask[x] = pick(hot, jnp.ones((columns, fine), BF))

    def hidden_layer(x):
        parts = []
        for a in (-1, 0, 1):
            for b in (-1, 0, 1):
                parts.append(s_buf[x + 1 + a, (1 + b) * NZ : (1 + b) * NZ + LAYER, :])
        total = lax.dot_general(jnp.concatenate(parts, axis=1), wf[...], NT, preferred_element_type=F32)
        total = jnp.where(mask[x // EDGE][:, 0:wide] > 0.5, jnp.maximum(total, 0.0), 0.0)
        packed = jnp.concatenate([total[j * rows : (j + 1) * rows] for j in range(n_chan)], axis=1)
        g_buf[x + 1, me] = packed.astype(BF)

    def send_layer(x):
        for k, chan in enumerate(peers):
            rc(g_buf.at[x + 1, me], g_buf.at[x + 1, me], s2.at[x, k], r2.at[x, me], sp, chan).start()

    early = NX // 2
    for load in loads[4:6]:
        load.wait()
    for x in range(1, early):
        hidden_layer(x)

    pl.semaphore_wait(
        barrier, n_chan - 1 + n_chan * (has_prev.astype(jnp.int32) + has_next.astype(jnp.int32))
    )

    up_feat = rc(feat.at[:, pl.ds((EDGE - 1) * FACE, FACE), :], fh.at[0], s1.at[0, 0], r1.at[0, 0], sp + 1, me)
    up_meta = rc(meta, mh.at[0], s1.at[0, 1], r1.at[0, 1], sp + 1, me)
    dn_feat = rc(feat.at[:, pl.ds(0, FACE), :], fh.at[1], s1.at[1, 0], r1.at[1, 0], sp - 1, me)
    dn_meta = rc(meta, mh.at[1], s1.at[1, 1], r1.at[1, 1], sp - 1, me)

    @pl.when(has_next)
    def _():
        up_meta.start()
        up_feat.start()

    @pl.when(has_prev)
    def _():
        dn_meta.start()
        dn_feat.start()

    for x in range(1, early):
        send_layer(x)
    for x in range(early, NX - 1):
        hidden_layer(x)
        send_layer(x)

    lane_par = jnp.where(
        iota((lanes, parents * cells), 1) // cells == iota((lanes, parents * cells), 0), 1.0, 0.0
    )

    def dest_table(k):
        block = meta[...] if k == 1 else mh[k // 2]
        rel = jnp.dot(block.astype(F32), lane_par, preferred_element_type=F32)[1:2].astype(jnp.int32)
        slot = rel - (2 - k) * slots
        target = slot * cells + iota((1, parents * cells), 1) % cells
        ids = iota((slots * cells, parents * cells), 0)
        ohd[k] = one(ids == jnp.where((slot >= 0) & (slot < slots), target, -1))

    dest_table(1)

    def halo_layer(side):
        k = keys_of(mh[side])
        block = fh[side].reshape(columns, fine)
        for c in (-1, 0, 1):
            s_buf[0 if side == 0 else NX + 1, NZ : NZ + LAYER, (c + 1) * fine : (c + 2) * fine] = pick(
                one_hot(k, 1 - side, c), block
            ).astype(BF)

    @pl.when(has_next)
    def _():
        dn_meta.wait_recv()
        dn_feat.wait_recv()

    halo_layer(1)
    hidden_layer(NX - 1)

    @pl.when(has_next)
    def _():
        for chan in range(n_chan):
            rc(g_buf.at[NX, me], g_buf.at[0, me], hs2.at[chan], hr2.at[me], sp + 1, chan).start()

    send_layer(NX - 1)

    @pl.when(has_prev)
    def _():
        up_meta.wait_recv()
        up_feat.wait_recv()

    halo_layer(0)
    hidden_layer(0)
    send_layer(0)

    def wait_layer(x):
        for k in range(1, n_chan):
            src = lax.rem(me + k, n_chan)
            rc(g_buf.at[x + 1, src], g_buf.at[x + 1, src], s2.at[x, 0], r2.at[x, src], sp, src).wait_recv()

    def spread_layers(buf, at, perm, height, width, parts):
        gathered = jnp.concatenate(
            [jnp.concatenate([buf[x, s] for s in range(n_chan)], axis=1) for x in at], axis=0
        )
        moved = pick(gathered, perm[...]).astype(BF)
        layers = [
            jnp.concatenate(
                [moved[i * height : (i + 1) * height, j * width : (j + 1) * width] for j in range(parts)],
                axis=0,
            )
            for i in range(len(at))
        ]
        return jnp.concatenate(layers, axis=1)

    def fill_d(at):
        filled = pick(sel_d[...], spread_layers(g_buf, at, perm_h, rows, fine, n_chan)).astype(BF)
        for i, x in enumerate(at):
            d_buf[:, x * fine : (x + 1) * fine] = filled[:, i * fine : (i + 1) * fine]

    def down(at):
        stacked = []
        for x in at:
            stacked.append(
                jnp.concatenate(
                    [
                        d_buf[bc * CLAYER : (bc + 1) * CLAYER, (2 * x + a) * fine : (2 * x + a + 1) * fine]
                        for a in range(3)
                        for bc in range(taps2)
                    ],
                    axis=1,
                )
            )
        pieces = lax.dot_general(jnp.concatenate(stacked, axis=0), wd[...], NT, preferred_element_type=F32)
        for i, x in enumerate(at):
            live = pick(sel_d[4 * CLAYER : 5 * CLAYER, :], mask[x // 2].astype(BF))[:, 0:coarse_own]
            part = pieces[i * CLAYER : (i + 1) * CLAYER]
            part = jnp.where(live > 0.5, jnp.maximum(part, 0.0), 0.0)
            c_buf[x + 1, me] = jnp.concatenate(
                [part[j * crows : (j + 1) * crows] for j in range(half)], axis=1
            ).astype(BF)

    inner = list(range(1, CX - 1))
    for load in loads[6:9]:
        load.wait()
    for x in range(1, NX - 1):
        wait_layer(x)
    fill_d(list(range(2, NX)))
    down(inner)

    @pl.when(has_prev)
    def _():
        for chan in range(n_chan):
            rc(g_buf.at[0, chan], g_buf.at[0, chan], hs2.at[chan], hr2.at[chan], sp - 1, chan).wait_recv()

    wait_layer(NX - 1)
    wait_layer(0)
    fill_d([0, 1, NX])
    down([0, CX - 1])

    @pl.when(has_next)
    def _():
        for chan in range(n_chan):
            rc(c_buf.at[CX, me], c_buf.at[0, me], hs3.at[0, chan], hr3.at[0, me], sp + 1, chan).start()

    @pl.when(has_prev)
    def _():
        for chan in range(n_chan):
            rc(c_buf.at[1, me], c_buf.at[CX + 1, me], hs3.at[1, chan], hr3.at[1, me], sp - 1, chan).start()

    own_c = c_buf.at[pl.ds(1, CX), me]
    for k, chan in enumerate(peers):
        rc(own_c, own_c, s3.at[k], r3.at[me], sp, chan).start()

    dest_table(0)
    dest_table(2)
    for load in loads[9:]:
        load.wait()

    for k in range(1, n_chan):
        src = lax.rem(me + k, n_chan)
        ref = c_buf.at[pl.ds(1, CX), src]
        rc(ref, ref, s3.at[0], r3.at[src], sp, src).wait_recv()

    def fill_e(at):
        filled = pick(sel_c[...], spread_layers(c_buf, at, perm_c, crows, coarse, half)).astype(BF)
        for i, x in enumerate(at):
            e_buf[:, x * coarse : (x + 1) * coarse] = filled[:, i * coarse : (i + 1) * coarse]

    def coarse_taps(a, total):
        for bc in range(taps2):
            block = jnp.concatenate(
                [
                    e_buf[
                        bc * CLAYER + g * FACE : bc * CLAYER + (g + 1) * FACE,
                        (x + a) * coarse : (x + a + 1) * coarse,
                    ]
                    for g in range(parents)
                    for x in range(CX)
                ],
                axis=0,
            )
            t = a * taps2 + bc
            term = lax.dot_general(wc[:, t * coarse : (t + 1) * coarse], block, NT, preferred_element_type=F32)
            total = term if total is None else total + term
        return total

    fill_e(list(range(1, CX + 1)))
    total = coarse_taps(1, None)

    @pl.when(has_prev)
    def _():
        for chan in range(n_chan):
            ref = c_buf.at[0, chan]
            rc(ref, ref, hs3.at[0, chan], hr3.at[0, chan], sp - 1, chan).wait_recv()

    @pl.when(has_next)
    def _():
        for chan in range(n_chan):
            ref = c_buf.at[CX + 1, chan]
            rc(ref, ref, hs3.at[1, chan], hr3.at[1, chan], sp + 1, chan).wait_recv()

    fill_e([0, CX + 1])
    total = coarse_taps(0, total)
    total = coarse_taps(2, total)
    rounded = total.astype(BF)
    pb[1] = rounded
    values = rounded.astype(F32)
    pw[1, me] = jnp.sum(values * values, axis=0, keepdims=True)

    for k, chan in enumerate(peers):
        rc(pw.at[1, me], pw.at[1, me], ws4.at[1, k], wr4.at[1, me], sp, chan).start()

    @pl.when(has_next)
    def _():
        rc(pb.at[1], pb.at[0], s4.at[0], r4.at[0], sp + 1, me).start()
        for chan in range(n_chan):
            rc(pw.at[1, me], pw.at[0, me], ws4.at[0, chan], wr4.at[0, me], sp + 1, chan).start()

    @pl.when(has_prev)
    def _():
        rc(pb.at[1], pb.at[2], s4.at[1], r4.at[1], sp - 1, me).start()
        for chan in range(n_chan):
            rc(pw.at[1, me], pw.at[2, me], ws4.at[2, chan], wr4.at[2, me], sp - 1, chan).start()

    own = gain.shape[1]
    gain_col = jnp.sum(
        jnp.where(iota((own, own), 0) == iota((own, own), 1), gain[...], 0.0), axis=1, keepdims=True
    )

    def normed(k):
        power = pw[k, 0]
        for s in range(1, n_chan):
            power = power + pw[k, s]
        scaled = pb[k].astype(F32) * lax.rsqrt(power / coarse + epsilon) * gain_col
        return lax.dot_general(scaled.astype(BF), ohd[k], NT, preferred_element_type=F32)

    for k in range(1, n_chan):
        src = lax.rem(me + k, n_chan)
        rc(pw.at[1, src], pw.at[1, src], ws4.at[1, 0], wr4.at[1, src], sp, src).wait_recv()
    result = normed(1)

    @pl.when(has_prev)
    def _():
        rc(pb.at[0], pb.at[0], s4.at[0], r4.at[0], sp - 1, me).wait_recv()
        for chan in range(n_chan):
            rc(pw.at[0, chan], pw.at[0, chan], ws4.at[0, chan], wr4.at[0, chan], sp - 1, chan).wait_recv()

    @pl.when(has_next)
    def _():
        rc(pb.at[2], pb.at[2], s4.at[1], r4.at[1], sp + 1, me).wait_recv()
        for chan in range(n_chan):
            rc(pw.at[2, chan], pw.at[2, chan], ws4.at[2, chan], wr4.at[2, chan], sp + 1, chan).wait_recv()

    out[...] = (result + normed(0) + normed(2)).astype(BF)

    for x in range(NX):
        for k, chan in enumerate(peers):
            rc(g_buf.at[x + 1, me], g_buf.at[x + 1, me], s2.at[x, k], r2.at[x, me], sp, chan).wait_send()
    for k, chan in enumerate(peers):
        rc(own_c, own_c, s3.at[k], r3.at[me], sp, chan).wait_send()
        rc(pw.at[1, me], pw.at[1, me], ws4.at[1, k], wr4.at[1, me], sp, chan).wait_send()

    @pl.when(has_next)
    def _():
        up_meta.wait_send()
        up_feat.wait_send()
        rc(pb.at[1], pb.at[0], s4.at[0], r4.at[0], sp + 1, me).wait_send()
        for chan in range(n_chan):
            rc(g_buf.at[NX, me], g_buf.at[0, me], hs2.at[chan], hr2.at[me], sp + 1, chan).wait_send()
            rc(c_buf.at[CX, me], c_buf.at[0, me], hs3.at[0, chan], hr3.at[0, me], sp + 1, chan).wait_send()
            rc(pw.at[1, me], pw.at[0, me], ws4.at[0, chan], wr4.at[0, me], sp + 1, chan).wait_send()

    @pl.when(has_prev)
    def _():
        dn_meta.wait_send()
        dn_feat.wait_send()
        rc(pb.at[1], pb.at[2], s4.at[1], r4.at[1], sp - 1, me).wait_send()
        for chan in range(n_chan):
            rc(c_buf.at[1, me], c_buf.at[CX + 1, me], hs3.at[1, chan], hr3.at[1, me], sp - 1, chan).wait_send()
            rc(pw.at[1, me], pw.at[2, me], ws4.at[2, chan], wr4.at[2, me], sp - 1, chan).wait_send()


def body(n_space, n_chan, features, neighbours, parent_index, octant, parent_dest, conv_fine, conv_down, conv_coarse, norm_gain):
    bricks, _, fine = features.shape
    parents = parent_dest.shape[0]
    slots = 2 * parents
    down = conv_down.shape[0]
    own = conv_coarse.shape[0]
    cells = EDGE**3
    coarse = down * n_chan
    vmem = pl.BlockSpec(memory_space=pltpu.VMEM)
    hbm = pl.BlockSpec(memory_space=pltpu.HBM)
    dma = pltpu.SemaphoreType.DMA
    big = n_chan * fine
    crows = CLAYER // (fine // down)
    return pl.pallas_call(
        functools.partial(fused_kernel, n_space, n_chan, bricks, slots),
        out_shape=jax.ShapeDtypeStruct((own, slots * cells), BF),
        in_specs=[hbm] * 12,
        out_specs=vmem,
        scratch_shapes=[
            pltpu.VMEM(features.shape, BF),
            pltpu.VMEM(conv_fine.shape, BF),
            pltpu.VMEM((1, own), F32),
            pltpu.VMEM((1, bricks), jnp.int32),
            pltpu.VMEM((1, bricks), jnp.int32),
            pltpu.VMEM((1, parents), jnp.int32),
            pltpu.VMEM((8, 128), jnp.int32),
            pltpu.VMEM(conv_down.shape, BF),
            pltpu.VMEM(conv_coarse.shape, BF),
            pltpu.VMEM((2, bricks, FACE, fine), BF),
            pltpu.VMEM((2, 8, 128), jnp.int32),
            pltpu.VMEM((NX + 2, LAYER + 2 * NZ, 3 * fine), BF),
            pltpu.VMEM((2, LAYER, fine), F32),
            pltpu.VMEM((NX + 1, n_chan, LAYER // n_chan, fine), BF),
            pltpu.VMEM((big, big), BF),
            pltpu.VMEM((big, big), BF),
            pltpu.VMEM((9 * CLAYER, LAYER), BF),
            pltpu.VMEM((9 * CLAYER, CLAYER), BF),
            pltpu.VMEM((9 * CLAYER, (NX + 1) * fine), BF),
            pltpu.VMEM((CX + 2, n_chan, crows, fine), BF),
            pltpu.VMEM((9 * CLAYER, (CX + 2) * coarse), BF),
            pltpu.VMEM((3, own, parents * cells), BF),
            pltpu.VMEM((3, n_chan, 1, parents * cells), F32),
            pltpu.VMEM((3, slots * cells, parents * cells), BF),
            dma((12,)),
            dma((2, 2)),
            dma((2, 2)),
            dma((NX, n_chan - 1)),
            dma((NX, n_chan)),
            dma((n_chan,)),
            dma((n_chan,)),
            dma((n_chan - 1,)),
            dma((n_chan,)),
            dma((2, n_chan)),
            dma((2, n_chan)),
            dma((2,)),
            dma((2,)),
            dma((3, n_chan)),
            dma((3, n_chan)),
        ],
        compiler_params=pltpu.CompilerParams(collective_id=0, has_side_effects=True, vmem_limit_bytes=66900000
        ),
    )(
        features,
        parent_index.reshape(1, -1),
        octant.reshape(1, -1),
        parent_dest.reshape(1, -1),
        conv_fine,
        conv_down,
        conv_coarse,
        norm_gain.reshape(1, -1),
        *tables(n_chan, fine, down),
    )


def solution(mesh):
    sizes = dict(mesh.shape)
    return jax.shard_map(
        functools.partial(body, sizes["space"], sizes["chan"]),
        mesh=mesh,
        in_specs=(
            P("space", None, None),
            P("space", None),
            P("space"),
            P("space"),
            P("space"),
            P("chan", None),
            P("chan", None),
            P("chan", None),
            P("chan"),
        ),
        out_specs=P("chan", "space"),
        check_vma=False,
    )
```

```python
import functools

import jax
import jax.numpy as jnp
import numpy as np
from jax import lax
from jax.experimental import pallas as pl
from jax.experimental.pallas import tpu as pltpu
from jax.sharding import PartitionSpec as P

EDGE = 4
SLAB_Y = 4
SLAB_Z = 4
NY = SLAB_Y * EDGE
NZ = SLAB_Z * EDGE
LAYER = NY * NZ
NX = 2 * EDGE
CY = NY // 2
CZ = NZ // 2
CLAYER = CY * CZ
CX = NX // 2
FACE = EDGE * EDGE
epsilon = 1e-06
BF = jnp.bfloat16
F32 = jnp.float32
NT = (((1,), (1,)), ((), ()))


def iota(shape, dim):
    return lax.broadcasted_iota(jnp.int32, shape, dim)


def one(cond):
    return jnp.where(cond, 1.0, 0.0).astype(BF)


def pick(a, b):
    return jnp.dot(a, b, preferred_element_type=F32)


def tables(n_chan, fine, coarse_own):
    def held(cond):
        return jnp.asarray(np.asarray(cond, np.float32).astype(jnp.bfloat16))

    def grid(rows, columns):
        return np.arange(rows)[:, None], np.arange(columns)[None, :]

    wide = fine // n_chan
    coarse = coarse_own * n_chan
    r, q = grid(n_chan * fine, n_chan * fine)
    perm_h = held((r % fine) // wide * fine + r // fine * wide + r % wide == q)
    perm_c = held((r % fine) // coarse_own * coarse + r // fine * coarse_own + r % coarse_own == q)
    r, q = grid(9 * CLAYER, LAYER)
    bc, at = r // CLAYER, r % CLAYER
    y = 2 * (at // CZ) + bc // 3 - 1
    z = 2 * (at % CZ) + bc % 3 - 1
    sel_d = held((y >= 0) & (z >= 0) & (y * NZ + z == q))
    r, q = grid(9 * CLAYER, CLAYER)
    bc, at = r // CLAYER, r % CLAYER
    par, yz = at // FACE, at % FACE
    y = par // (SLAB_Z // 2) * EDGE + yz // EDGE + bc // 3 - 1
    z = par % (SLAB_Z // 2) * EDGE + yz % EDGE + bc % 3 - 1
    sel_c = held((y >= 0) & (z >= 0) & (z < CZ) & (y * CZ + z == q))
    return perm_h, perm_c, sel_d, sel_c


def fused_kernel(
    n_space, n_chan, bricks, slots,
    feat_hbm, parent_hbm, octant_hbm, dest_hbm, wf_hbm, wd_hbm, wc_hbm, gain_hbm,
    perm_h_hbm, perm_c_hbm, sel_d_hbm, sel_c_hbm,
    out,
    feat, wf, gain, parent_in, octant_in, dest_in, meta, wd, wc, fh, mh, s_buf, mask, g_buf,
    perm_h, perm_c, sel_d, sel_c, d_buf, c_buf, e_buf, pb, pw, ohd, hot0, hot_t, sel_x,
    wsem, s1, r1, s2, r2, hs2, hr2, s3, r3, hs3, hr3, s4, r4, ws4, wr4,
):
    sp = lax.axis_index("space")
    me = lax.axis_index("chan")
    has_prev = sp > 0
    has_next = sp < n_space - 1
    fine = feat.shape[2]
    wide = fine // n_chan
    parents = dest_in.shape[1]
    cells = EDGE**3
    coarse_own = wd.shape[0]
    coarse = coarse_own * n_chan
    taps2 = 9
    half = fine // coarse_own
    crows = CLAYER // half
    rows = bricks * FACE // n_chan

    def rc(src, dst, ss, rs, space, chan):
        return pltpu.make_async_remote_copy(
            src_ref=src,
            dst_ref=dst,
            send_sem=ss,
            recv_sem=rs,
            device_id={"space": space, "chan": chan},
            device_id_type=pl.DeviceIdType.MESH,
        )

    peers = [lax.rem(me + k, n_chan) for k in range(1, n_chan)]
    barrier = pltpu.get_barrier_semaphore()

    def greet(space, chan):
        pl.semaphore_signal(
            barrier,
            inc=1,
            device_id={"space": space, "chan": chan},
            device_id_type=pl.DeviceIdType.MESH,
        )

    @pl.when(has_prev)
    def _():
        for chan in range(n_chan):
            greet(sp - 1, chan)

    @pl.when(has_next)
    def _():
        for chan in range(n_chan):
            greet(sp + 1, chan)

    for chan in peers:
        greet(sp, chan)

    loads = [
        pltpu.make_async_copy(src, dst, wsem.at[k])
        for k, (src, dst) in enumerate(
            (
                (parent_hbm, parent_in),
                (octant_hbm, octant_in),
                (dest_hbm, dest_in),
                (feat_hbm, feat),
                (wf_hbm, wf),
                (gain_hbm, gain),
                (perm_h_hbm, perm_h),
                (sel_d_hbm, sel_d),
                (wd_hbm, wd),
                (perm_c_hbm, perm_c),
                (sel_c_hbm, sel_c),
                (wc_hbm, wc),
            )
        )
    ]
    for load in loads:
        load.start()

    @pl.when(jnp.logical_not(has_prev))
    def _():
        fh[0] = jnp.zeros(fh.shape[1:], BF)
        mh[0] = jnp.zeros(mh.shape[1:], jnp.int32)
        g_buf[0] = jnp.zeros(g_buf.shape[1:], BF)
        c_buf[0] = jnp.zeros(c_buf.shape[1:], BF)
        pb[0] = jnp.zeros(pb.shape[1:], BF)
        pw[0] = jnp.zeros(pw.shape[1:], F32)

    @pl.when(jnp.logical_not(has_next))
    def _():
        fh[1] = jnp.zeros(fh.shape[1:], BF)
        mh[1] = jnp.zeros(mh.shape[1:], jnp.int32)
        c_buf[CX + 1] = jnp.zeros(c_buf.shape[1:], BF)
        pb[2] = jnp.zeros(pb.shape[1:], BF)
        pw[2] = jnp.zeros(pw.shape[1:], F32)

    blank_y = jnp.zeros((NX + 2, NZ, 3 * fine), BF)
    s_buf[:, 0:NZ, :] = blank_y
    s_buf[:, NZ + LAYER : 2 * NZ + LAYER, :] = blank_y

    lanes = meta.shape[1]
    columns = bricks * FACE
    spread = jnp.where(iota((lanes, columns), 1) // FACE == iota((lanes, columns), 0), 1.0, 0.0)
    face = iota((1, columns), 1) % FACE
    row_ids = iota((LAYER, columns), 0)

    meta[...] = jnp.zeros(meta.shape, jnp.int32)
    for load in loads[:4]:
        load.wait()
    local = parent_in[...] - sp * parents
    octant = octant_in[...]
    y_pos = 2 * (local // (SLAB_Z // 2)) + octant // 2 % 2
    z_pos = 2 * (local % (SLAB_Z // 2)) + octant // 4
    meta[0:1, 0:bricks] = octant % 2 + 2 * y_pos + 2 * SLAB_Y * z_pos
    meta[1:2, 0:parents] = dest_in[...] - (sp - 1) * slots

    def keys_of(meta_block):
        code = jnp.dot(meta_block.astype(F32), spread, preferred_element_type=F32)[0:1].astype(jnp.int32)
        x_bit = code % 2
        y_pos = code // 2 % SLAB_Y
        z_pos = code // (2 * SLAB_Y)
        y = y_pos * EDGE + face // EDGE
        z = z_pos * EDGE + face % EDGE
        return x_bit, y, z

    def one_hot(key, x_want, c):
        x_bit, y, z = key
        fits = (x_bit == x_want) & (z - c >= 0) & (z - c < NZ)
        return one(row_ids == jnp.where(fits, y * NZ + z - c, -1))

    faces = jnp.concatenate(
        [feat[:, i * FACE : (i + 1) * FACE, :].reshape(columns, fine) for i in range(EDGE)], axis=1
    )
    key = keys_of(meta[...])
    for x in range(2):
        for c in (-1, 0, 1):
            hot = one_hot(key, x, c)
            placed = pick(hot, faces).astype(BF)
            for i in range(EDGE):
                s_buf[1 + EDGE * x + i, NZ : NZ + LAYER, (c + 1) * fine : (c + 2) * fine] = placed[
                    :, i * fine : (i + 1) * fine
                ]
            if c == 0:
                mask[x] = pick(hot, jnp.ones((columns, fine), BF))
                hot0[x] = hot
                hot_t[:, x * LAYER : (x + 1) * LAYER] = hot.astype(F32).T.astype(BF)

    def hidden_layer(x):
        parts = []
        for a in (-1, 0, 1):
            for b in (-1, 0, 1):
                parts.append(s_buf[x + 1 + a, (1 + b) * NZ : (1 + b) * NZ + LAYER, :])
        total = lax.dot_general(jnp.concatenate(parts, axis=1), wf[...], NT, preferred_element_type=F32)
        return jnp.maximum(total, 0.0).astype(BF)

    def pack(i, low, high):
        total = pick(hot_t[...], jnp.concatenate([low, high], axis=0))
        packed = jnp.concatenate([total[j * rows : (j + 1) * rows] for j in range(n_chan)], axis=1)
        g_buf[i + 1, me] = packed.astype(BF)

    def send_layer(i):
        for k, chan in enumerate(peers):
            rc(g_buf.at[i + 1, me], g_buf.at[i + 1, me], s2.at[i, k], r2.at[i, me], sp, chan).start()

    for load in loads[4:6]:
        load.wait()
    pack(1, hidden_layer(1), hidden_layer(EDGE + 1))
    early = hidden_layer(2)

    pl.semaphore_wait(
        barrier, n_chan - 1 + n_chan * (has_prev.astype(jnp.int32) + has_next.astype(jnp.int32))
    )

    up_feat = rc(feat.at[:, pl.ds((EDGE - 1) * FACE, FACE), :], fh.at[0], s1.at[0, 0], r1.at[0, 0], sp + 1, me)
    up_meta = rc(meta, mh.at[0], s1.at[0, 1], r1.at[0, 1], sp + 1, me)
    dn_feat = rc(feat.at[:, pl.ds(0, FACE), :], fh.at[1], s1.at[1, 0], r1.at[1, 0], sp - 1, me)
    dn_meta = rc(meta, mh.at[1], s1.at[1, 1], r1.at[1, 1], sp - 1, me)

    @pl.when(has_next)
    def _():
        up_meta.start()
        up_feat.start()

    @pl.when(has_prev)
    def _():
        dn_meta.start()
        dn_feat.start()

    send_layer(1)
    pack(2, early, hidden_layer(EDGE + 2))
    send_layer(2)
    third = hidden_layer(EDGE - 1)
    fourth = hidden_layer(EDGE)

    lane_par = jnp.where(
        iota((lanes, parents * cells), 1) // cells == iota((lanes, parents * cells), 0), 1.0, 0.0
    )

    def dest_table(k):
        block = meta[...] if k == 1 else mh[k // 2]
        rel = jnp.dot(block.astype(F32), lane_par, preferred_element_type=F32)[1:2].astype(jnp.int32)
        slot = rel - (2 - k) * slots
        target = slot * cells + iota((1, parents * cells), 1) % cells
        ids = iota((slots * cells, parents * cells), 0)
        ohd[k] = one(ids == jnp.where((slot >= 0) & (slot < slots), target, -1))

    dest_table(1)
    for load in loads[6:9]:
        load.wait()
    for x in range(2):
        sel_x[x] = pick(sel_d[...], hot0[x]).astype(BF)

    def halo_layer(side):
        k = keys_of(mh[side])
        block = fh[side].reshape(columns, fine)
        for c in (-1, 0, 1):
            hot = one_hot(k, 1 - side, c)
            s_buf[0 if side == 0 else NX + 1, NZ : NZ + LAYER, (c + 1) * fine : (c + 2) * fine] = pick(
                hot, block
            ).astype(BF)
            if side == 0 and c == 0:
                sel_x[2] = pick(sel_d[...], hot).astype(BF)

    @pl.when(has_next)
    def _():
        dn_meta.wait_recv()
        dn_feat.wait_recv()

    halo_layer(1)
    pack(EDGE - 1, third, hidden_layer(NX - 1))

    @pl.when(has_next)
    def _():
        for chan in range(n_chan):
            rc(g_buf.at[EDGE, me], g_buf.at[0, me], hs2.at[chan], hr2.at[me], sp + 1, chan).start()

    send_layer(EDGE - 1)

    @pl.when(has_prev)
    def _():
        up_meta.wait_recv()
        up_feat.wait_recv()

    halo_layer(0)
    pack(0, hidden_layer(0), fourth)
    send_layer(0)

    def wait_layer(x):
        for k in range(1, n_chan):
            src = lax.rem(me + k, n_chan)
            rc(g_buf.at[x + 1, src], g_buf.at[x + 1, src], s2.at[x, 0], r2.at[x, src], sp, src).wait_recv()

    def spread_layers(buf, at, perm, height, width, parts):
        gathered = jnp.concatenate(
            [jnp.concatenate([buf[x, s] for s in range(n_chan)], axis=1) for x in at], axis=0
        )
        moved = pick(gathered, perm[...]).astype(BF)
        layers = [
            jnp.concatenate(
                [moved[i * height : (i + 1) * height, j * width : (j + 1) * width] for j in range(parts)],
                axis=0,
            )
            for i in range(len(at))
        ]
        return jnp.concatenate(layers, axis=1)

    def fill_d(at):
        moved = spread_layers(g_buf, [i + 1 for i in at], perm_h, rows, fine, n_chan)
        owned = [k for k, i in enumerate(at) if i >= 0]
        for x in range(3):
            kept = owned if x < 2 else [k for k, i in enumerate(at) if i < 0]
            if not kept:
                continue
            block = jnp.concatenate([moved[:, k * fine : (k + 1) * fine] for k in kept], axis=1)
            filled = pick(sel_x[x], block).astype(BF)
            for n, k in enumerate(kept):
                at_x = 1 + EDGE * x + at[k] if x < 2 else 0
                d_buf[:, at_x * fine : (at_x + 1) * fine] = filled[:, n * fine : (n + 1) * fine]

    def down(at):
        stacked = []
        for x in at:
            stacked.append(
                jnp.concatenate(
                    [
                        d_buf[bc * CLAYER : (bc + 1) * CLAYER, (2 * x + a) * fine : (2 * x + a + 1) * fine]
                        for a in range(3)
                        for bc in range(taps2)
                    ],
                    axis=1,
                )
            )
        pieces = lax.dot_general(jnp.concatenate(stacked, axis=0), wd[...], NT, preferred_element_type=F32)
        for i, x in enumerate(at):
            live = pick(sel_d[4 * CLAYER : 5 * CLAYER, :], mask[x // 2].astype(BF))[:, 0:coarse_own]
            part = pieces[i * CLAYER : (i + 1) * CLAYER]
            part = jnp.where(live > 0.5, jnp.maximum(part, 0.0), 0.0)
            c_buf[x + 1, me] = jnp.concatenate(
                [part[j * crows : (j + 1) * crows] for j in range(half)], axis=1
            ).astype(BF)

    wait_layer(1)
    wait_layer(2)
    fill_d([1, 2])

    @pl.when(has_prev)
    def _():
        for chan in range(n_chan):
            rc(g_buf.at[0, chan], g_buf.at[0, chan], hs2.at[chan], hr2.at[chan], sp - 1, chan).wait_recv()

    wait_layer(EDGE - 1)
    wait_layer(0)
    fill_d([-1, 0, EDGE - 1])
    down(range(CX))

    @pl.when(has_next)
    def _():
        for chan in range(n_chan):
            rc(c_buf.at[CX, me], c_buf.at[0, me], hs3.at[0, chan], hr3.at[0, me], sp + 1, chan).start()

    @pl.when(has_prev)
    def _():
        for chan in range(n_chan):
            rc(c_buf.at[1, me], c_buf.at[CX + 1, me], hs3.at[1, chan], hr3.at[1, me], sp - 1, chan).start()

    own_c = c_buf.at[pl.ds(1, CX), me]
    for k, chan in enumerate(peers):
        rc(own_c, own_c, s3.at[k], r3.at[me], sp, chan).start()

    dest_table(0)
    dest_table(2)
    for load in loads[9:]:
        load.wait()

    for k in range(1, n_chan):
        src = lax.rem(me + k, n_chan)
        ref = c_buf.at[pl.ds(1, CX), src]
        rc(ref, ref, s3.at[0], r3.at[src], sp, src).wait_recv()

    def fill_e(at):
        filled = pick(sel_c[...], spread_layers(c_buf, at, perm_c, crows, coarse, half)).astype(BF)
        for i, x in enumerate(at):
            e_buf[:, x * coarse : (x + 1) * coarse] = filled[:, i * coarse : (i + 1) * coarse]

    def coarse_taps(a, total):
        for bc in range(taps2):
            block = jnp.concatenate(
                [
                    e_buf[
                        bc * CLAYER + g * FACE : bc * CLAYER + (g + 1) * FACE,
                        (x + a) * coarse : (x + a + 1) * coarse,
                    ]
                    for g in range(parents)
                    for x in range(CX)
                ],
                axis=0,
            )
            t = a * taps2 + bc
            term = lax.dot_general(wc[:, t * coarse : (t + 1) * coarse], block, NT, preferred_element_type=F32)
            total = term if total is None else total + term
        return total

    fill_e(list(range(1, CX + 1)))
    total = coarse_taps(1, None)

    @pl.when(has_prev)
    def _():
        for chan in range(n_chan):
            ref = c_buf.at[0, chan]
            rc(ref, ref, hs3.at[0, chan], hr3.at[0, chan], sp - 1, chan).wait_recv()

    @pl.when(has_next)
    def _():
        for chan in range(n_chan):
            ref = c_buf.at[CX + 1, chan]
            rc(ref, ref, hs3.at[1, chan], hr3.at[1, chan], sp + 1, chan).wait_recv()

    fill_e([0, CX + 1])
    total = coarse_taps(0, total)
    total = coarse_taps(2, total)
    rounded = total.astype(BF)
    pb[1] = rounded
    values = rounded.astype(F32)
    pw[1, me] = jnp.sum(values * values, axis=0, keepdims=True)

    for k, chan in enumerate(peers):
        rc(pw.at[1, me], pw.at[1, me], ws4.at[1, k], wr4.at[1, me], sp, chan).start()

    @pl.when(has_next)
    def _():
        rc(pb.at[1], pb.at[0], s4.at[0], r4.at[0], sp + 1, me).start()
        for chan in range(n_chan):
            rc(pw.at[1, me], pw.at[0, me], ws4.at[0, chan], wr4.at[0, me], sp + 1, chan).start()

    @pl.when(has_prev)
    def _():
        rc(pb.at[1], pb.at[2], s4.at[1], r4.at[1], sp - 1, me).start()
        for chan in range(n_chan):
            rc(pw.at[1, me], pw.at[2, me], ws4.at[2, chan], wr4.at[2, me], sp - 1, chan).start()

    own = gain.shape[1]
    gain_col = jnp.sum(
        jnp.where(iota((own, own), 0) == iota((own, own), 1), gain[...], 0.0), axis=1, keepdims=True
    )

    def normed(k):
        power = pw[k, 0]
        for s in range(1, n_chan):
            power = power + pw[k, s]
        scaled = pb[k].astype(F32) * lax.rsqrt(power / coarse + epsilon) * gain_col
        return lax.dot_general(scaled.astype(BF), ohd[k], NT, preferred_element_type=F32)

    for k in range(1, n_chan):
        src = lax.rem(me + k, n_chan)
        rc(pw.at[1, src], pw.at[1, src], ws4.at[1, 0], wr4.at[1, src], sp, src).wait_recv()
    result = normed(1)

    @pl.when(has_prev)
    def _():
        rc(pb.at[0], pb.at[0], s4.at[0], r4.at[0], sp - 1, me).wait_recv()
        for chan in range(n_chan):
            rc(pw.at[0, chan], pw.at[0, chan], ws4.at[0, chan], wr4.at[0, chan], sp - 1, chan).wait_recv()

    @pl.when(has_next)
    def _():
        rc(pb.at[2], pb.at[2], s4.at[1], r4.at[1], sp + 1, me).wait_recv()
        for chan in range(n_chan):
            rc(pw.at[2, chan], pw.at[2, chan], ws4.at[2, chan], wr4.at[2, chan], sp + 1, chan).wait_recv()

    out[...] = (result + normed(0) + normed(2)).astype(BF)

    for x in range(EDGE):
        for k, chan in enumerate(peers):
            rc(g_buf.at[x + 1, me], g_buf.at[x + 1, me], s2.at[x, k], r2.at[x, me], sp, chan).wait_send()
    for k, chan in enumerate(peers):
        rc(own_c, own_c, s3.at[k], r3.at[me], sp, chan).wait_send()
        rc(pw.at[1, me], pw.at[1, me], ws4.at[1, k], wr4.at[1, me], sp, chan).wait_send()

    @pl.when(has_next)
    def _():
        up_meta.wait_send()
        up_feat.wait_send()
        rc(pb.at[1], pb.at[0], s4.at[0], r4.at[0], sp + 1, me).wait_send()
        for chan in range(n_chan):
            rc(g_buf.at[EDGE, me], g_buf.at[0, me], hs2.at[chan], hr2.at[me], sp + 1, chan).wait_send()
            rc(c_buf.at[CX, me], c_buf.at[0, me], hs3.at[0, chan], hr3.at[0, me], sp + 1, chan).wait_send()
            rc(pw.at[1, me], pw.at[0, me], ws4.at[0, chan], wr4.at[0, me], sp + 1, chan).wait_send()

    @pl.when(has_prev)
    def _():
        dn_meta.wait_send()
        dn_feat.wait_send()
        rc(pb.at[1], pb.at[2], s4.at[1], r4.at[1], sp - 1, me).wait_send()
        for chan in range(n_chan):
            rc(c_buf.at[1, me], c_buf.at[CX + 1, me], hs3.at[1, chan], hr3.at[1, me], sp - 1, chan).wait_send()
            rc(pw.at[1, me], pw.at[2, me], ws4.at[2, chan], wr4.at[2, me], sp - 1, chan).wait_send()


def body(n_space, n_chan, features, neighbours, parent_index, octant, parent_dest, conv_fine, conv_down, conv_coarse, norm_gain):
    bricks, _, fine = features.shape
    parents = parent_dest.shape[0]
    slots = 2 * parents
    down = conv_down.shape[0]
    own = conv_coarse.shape[0]
    cells = EDGE**3
    coarse = down * n_chan
    vmem = pl.BlockSpec(memory_space=pltpu.VMEM)
    hbm = pl.BlockSpec(memory_space=pltpu.HBM)
    dma = pltpu.SemaphoreType.DMA
    big = n_chan * fine
    crows = CLAYER // (fine // down)
    return pl.pallas_call(
        functools.partial(fused_kernel, n_space, n_chan, bricks, slots),
        out_shape=jax.ShapeDtypeStruct((own, slots * cells), BF),
        in_specs=[hbm] * 12,
        out_specs=vmem,
        scratch_shapes=[
            pltpu.VMEM(features.shape, BF),
            pltpu.VMEM(conv_fine.shape, BF),
            pltpu.VMEM((1, own), F32),
            pltpu.VMEM((1, bricks), jnp.int32),
            pltpu.VMEM((1, bricks), jnp.int32),
            pltpu.VMEM((1, parents), jnp.int32),
            pltpu.VMEM((8, 128), jnp.int32),
            pltpu.VMEM(conv_down.shape, BF),
            pltpu.VMEM(conv_coarse.shape, BF),
            pltpu.VMEM((2, bricks, FACE, fine), BF),
            pltpu.VMEM((2, 8, 128), jnp.int32),
            pltpu.VMEM((NX + 2, LAYER + 2 * NZ, 3 * fine), BF),
            pltpu.VMEM((2, LAYER, fine), F32),
            pltpu.VMEM((EDGE + 1, n_chan, bricks * FACE // n_chan, fine), BF),
            pltpu.VMEM((big, big), BF),
            pltpu.VMEM((big, big), BF),
            pltpu.VMEM((9 * CLAYER, LAYER), BF),
            pltpu.VMEM((9 * CLAYER, CLAYER), BF),
            pltpu.VMEM((9 * CLAYER, (NX + 1) * fine), BF),
            pltpu.VMEM((CX + 2, n_chan, crows, fine), BF),
            pltpu.VMEM((9 * CLAYER, (CX + 2) * coarse), BF),
            pltpu.VMEM((3, own, parents * cells), BF),
            pltpu.VMEM((3, n_chan, 1, parents * cells), F32),
            pltpu.VMEM((3, slots * cells, parents * cells), BF),
            pltpu.VMEM((2, LAYER, bricks * FACE), BF),
            pltpu.VMEM((bricks * FACE, 2 * LAYER), BF),
            pltpu.VMEM((3, 9 * CLAYER, bricks * FACE), BF),
            dma((12,)),
            dma((2, 2)),
            dma((2, 2)),
            dma((EDGE, n_chan - 1)),
            dma((EDGE, n_chan)),
            dma((n_chan,)),
            dma((n_chan,)),
            dma((n_chan - 1,)),
            dma((n_chan,)),
            dma((2, n_chan)),
            dma((2, n_chan)),
            dma((2,)),
            dma((2,)),
            dma((3, n_chan)),
            dma((3, n_chan)),
        ],
        compiler_params=pltpu.CompilerParams(collective_id=0, has_side_effects=True, vmem_limit_bytes=66900000
        ),
    )(
        features,
        parent_index.reshape(1, -1),
        octant.reshape(1, -1),
        parent_dest.reshape(1, -1),
        conv_fine,
        conv_down,
        conv_coarse,
        norm_gain.reshape(1, -1),
        *tables(n_chan, fine, down),
    )


def solution(mesh):
    sizes = dict(mesh.shape)
    return jax.shard_map(
        functools.partial(body, sizes["space"], sizes["chan"]),
        mesh=mesh,
        in_specs=(
            P("space", None, None),
            P("space", None),
            P("space"),
            P("space"),
            P("space"),
            P("chan", None),
            P("chan", None),
            P("chan", None),
            P("chan"),
        ),
        out_specs=P("chan", "space"),
        check_vma=False,
    )
```
